256 devices in a mesh: region: 8 (over y, core), sub: 32 (over x, z).
Axes of the slice: x: 4, y: 4, z: 8, core: 2. Of those that a mesh axis runs over, the one named last changes fastest.
Arguments:
- probes: bfloat16 [32, 3407872], P(None, ('region', 'sub')), may hold values from -6 to 6
- blocks: bfloat16 [26624, 3, 128, 128], P(('region', 'sub')), may hold values from -0.109375 to 0.109375
- col_slot: int32 [26624, 3], P(('region', 'sub')), may hold values from 0 to 127, as said below
- send_sub: int32 [256, 2, 8], P(('region', 'sub')), may hold values from -1 to 103, as said below
- send_reg: int32 [256, 2, 4], P(('region', 'sub')), may hold values from -1 to 103, as said below
- coeffs: float32 [9], replicated, may hold values from 0.3 to 1
Outputs:
- filtered: float32 [32, 3407872], P(None, ('region', 'sub'))
The draws below stay inside these ranges and needn't reach their ends.
Inputs may be any that keep to these rules, and one draw needn't show every extreme that they name: `col_slot`: entry 0 of each block row names the row's own block. Slots from 104 on name received blocks in this order: 8 from the lower sub neighbour, 8 from the upper sub neighbour, 4 from the lower region neighbour, 4 from the upper one; only received slots that the sender fills are named, and each of those is named by some row. send_sub[d, 0] lists rows sent to sub index one lower in the same region, send_sub[d, 1] to one higher: distinct rows first, then -1; devices at the ends of the sub axis send nothing outward; some list is full. send_reg[d, 0] lists rows sent to the same sub index in the region one lower, send_reg[d, 1] one higher: distinct rows first, then -1; the first and last regions send nothing outward; some list is full.
All inputs are finite; a program needn't handle non-finite values.
Results may differ from the reference program's by a relative error of at most 0.0065.
Values may be sent and summed in bfloat16 or wider, within the bound.
A program may use at most 128 MiB of HBM per device.

```python
import jax
import jax.numpy as jnp
import numpy as np
from jax import lax

BLK = 128
NNZ = 3
PROBES = 32
DEG = 8
ROWS_DEV = 104
HS = 8
HR = 4
BLOCK_ROWS = 26624
NODES = 3407872
N_REGION = 8
N_SUB = 32


def halo_plan(key):
    device_total = N_REGION * N_SUB
    device_ids = jnp.arange(device_total)
    sub_index = device_ids % N_SUB
    region_index = device_ids // N_SUB
    sub_counts = jax.random.randint(jax.random.fold_in(key, 1), (device_total, 2), 1, HS + 1)
    sub_counts = sub_counts.at[0, 1].set(HS).at[1, 0].set(HS)
    sub_counts = jnp.stack([jnp.where(sub_index == 0, 0, sub_counts[:, 0]), jnp.where(sub_index == N_SUB - 1, 0, sub_counts[:, 1])], 1)
    reg_counts = jax.random.randint(jax.random.fold_in(key, 2), (device_total, 2), 1, HR + 1)
    reg_counts = reg_counts.at[0, 1].set(HR).at[N_SUB, 0].set(HR)
    reg_counts = jnp.stack([jnp.where(region_index == 0, 0, reg_counts[:, 0]), jnp.where(region_index == N_REGION - 1, 0, reg_counts[:, 1])], 1)

    def row_lists(base_key, width, counts):
        keys = jax.random.split(base_key, device_total * 2)
        orders = jax.vmap(lambda one_key: jax.random.permutation(one_key, ROWS_DEV))(keys).reshape(device_total, 2, ROWS_DEV)
        rotate = ROWS_DEV - 1 - orders[0, :, 0]
        orders = orders.at[0].set((orders[0] + rotate[:, None]) % ROWS_DEV)
        position = jnp.arange(width)[None, None, :]
        return jnp.where(position < counts[:, :, None], orders[:, :, :width], -1).astype(jnp.int32)
    send_sub = row_lists(jax.random.fold_in(key, 3), HS, sub_counts)
    send_reg = row_lists(jax.random.fold_in(key, 4), HR, reg_counts)
    grid_sub = sub_counts.reshape(N_REGION, N_SUB, 2)
    grid_reg = reg_counts.reshape(N_REGION, N_SUB, 2)
    zero_column = jnp.zeros((N_REGION, 1), grid_sub.dtype)
    zero_row = jnp.zeros((1, N_SUB), grid_reg.dtype)
    recv_first = jnp.concatenate([zero_column, grid_sub[:, :-1, 1]], 1).reshape(device_total)
    recv_second = jnp.concatenate([grid_sub[:, 1:, 0], zero_column], 1).reshape(device_total)
    recv_third = jnp.concatenate([zero_row, grid_reg[:-1, :, 1]], 0).reshape(device_total)
    recv_fourth = jnp.concatenate([grid_reg[1:, :, 0], zero_row], 0).reshape(device_total)
    recv_counts = jnp.stack([recv_first, recv_second, recv_third, recv_fourth], 1)
    segment = np.array([0] * HS + [1] * HS + [2] * HR + [3] * HR, dtype=np.int32)
    inside = np.array(list(range(HS)) + list(range(HS)) + list(range(HR)) + list(range(HR)), dtype=np.int32)
    received = 2 * HS + 2 * HR
    live = jnp.asarray(inside)[None, :] < recv_counts[:, segment]
    extra_count = ROWS_DEV * (NNZ - 1)
    filler = jax.random.randint(jax.random.fold_in(key, 5), (device_total, extra_count), 0, ROWS_DEV)
    place_keys = jax.random.split(jax.random.fold_in(key, 6), device_total)
    places = jax.vmap(lambda one_key: jax.random.permutation(one_key, extra_count))(place_keys)[:, :received]
    chosen = jnp.where(live, ROWS_DEV + jnp.arange(received)[None, :], jnp.take_along_axis(filler, places, axis=1))
    extra = filler.at[device_ids[:, None], places].set(chosen)
    extra = extra.reshape(device_total, ROWS_DEV, NNZ - 1)
    own = jnp.broadcast_to(jnp.arange(ROWS_DEV)[None, :, None], (device_total, ROWS_DEV, 1))
    col_slot = jnp.concatenate([own, extra], 2).reshape(device_total * ROWS_DEV, NNZ).astype(jnp.int32)
    return (send_sub, send_reg, col_slot)


def draw_col_slot(key, part):
    return halo_plan(key)[2]


def draw_send_sub(key, part):
    return halo_plan(key)[0]


def draw_send_reg(key, part):
    return halo_plan(key)[1]


def block_levels(rng, shape, cuts, smallest, top_value):
    loudness, own = 1.0, jax.random.fold_in(rng, 6)
    for axis_at, parts in cuts:
        draws = jnp.exp(jax.random.uniform(jax.random.fold_in(own, axis_at), (parts,), jnp.float32, smallest / len(cuts), top_value / len(cuts)))
        loudness = loudness * jnp.repeat(draws, shape[axis_at] // parts).reshape([-1 if axis == axis_at else 1 for axis in range(len(shape))])
    return loudness


def noise(rng, extent, deviation, most, cuts=(), kind=jnp.bfloat16):
    drawn = deviation * jax.random.normal(rng, extent, jnp.float32)
    if cuts:
        drawn = drawn * block_levels(rng, extent, cuts, -0.22, 0.18)
    return jnp.clip(drawn, -most, most).astype(kind)


def setup_inputs(seed: int = 0) -> dict:
    key_of = jax.random.split(jax.random.key(seed), 7)
    probes = noise(key_of[0], (PROBES, NODES), 1.0, 6.0, ((1, 256),))
    blocks = noise(key_of[1], (BLOCK_ROWS, NNZ, BLK, BLK), (8 * NNZ * BLK) ** -0.5, 0.109375, ((0, 256),))
    col_slot = draw_col_slot(jax.random.fold_in(key_of[6], 71), 0)
    send_sub = draw_send_sub(jax.random.fold_in(key_of[6], 71), 0)
    send_reg = draw_send_reg(jax.random.fold_in(key_of[6], 71), 0)
    coeffs = jnp.clip(jax.random.uniform(key_of[5], (DEG + 1,), jnp.float32, 0.3, 1.0), 0.3, 1.0)
    return {"probes": probes, "blocks": blocks, "col_slot": col_slot, "send_sub": send_sub, "send_reg": send_reg, "coeffs": coeffs}


def column_ids(col_slot, send_sub, send_reg):
    device_total = N_REGION * N_SUB
    slots = col_slot.reshape(device_total, ROWS_DEV, NNZ)
    device_ids = jnp.arange(device_total, dtype=jnp.int32)[:, None, None]
    own_ids = device_ids * ROWS_DEV + slots
    lower_sub = jnp.clip(device_ids - 1, 0, device_total - 1)
    upper_sub = jnp.clip(device_ids + 1, 0, device_total - 1)
    lower_reg = jnp.clip(device_ids - N_SUB, 0, device_total - 1)
    upper_reg = jnp.clip(device_ids + N_SUB, 0, device_total - 1)
    offset = slots - ROWS_DEV
    first_pos = jnp.clip(offset, 0, HS - 1)
    second_pos = jnp.clip(offset - HS, 0, HS - 1)
    third_pos = jnp.clip(offset - 2 * HS, 0, HR - 1)
    fourth_pos = jnp.clip(offset - 2 * HS - HR, 0, HR - 1)
    first_ids = lower_sub * ROWS_DEV + send_sub[lower_sub, 1, first_pos]
    second_ids = upper_sub * ROWS_DEV + send_sub[upper_sub, 0, second_pos]
    third_ids = lower_reg * ROWS_DEV + send_reg[lower_reg, 1, third_pos]
    fourth_ids = upper_reg * ROWS_DEV + send_reg[upper_reg, 0, fourth_pos]
    result = jnp.where(offset < 2 * HS + HR, third_ids, fourth_ids)
    result = jnp.where(offset < 2 * HS, second_ids, result)
    result = jnp.where(offset < HS, first_ids, result)
    result = jnp.where(offset < 0, own_ids, result)
    return result.astype(jnp.int32)


def apply_operator(packed, blocks_dev, global_ids):
    vectors = packed.reshape(PROBES, BLOCK_ROWS, BLK)

    def one_device(items):
        block_group, id_group = items
        taken = jnp.take(vectors, id_group, axis=1)
        return jnp.einsum("pnkc,nkac->pna", taken.astype(jnp.float32), block_group.astype(jnp.float32))

    result = lax.map(one_device, (blocks_dev, global_ids))
    return jnp.transpose(result, (1, 0, 2, 3)).reshape(PROBES, NODES)


def reference(probes, blocks, col_slot, send_sub, send_reg, coeffs):
    device_total = N_REGION * N_SUB
    global_ids = column_ids(col_slot, send_sub, send_reg)
    blocks_dev = blocks.reshape(device_total, ROWS_DEV, NNZ, BLK, BLK)
    previous = probes.astype(jnp.float32)
    total = coeffs[0] * previous
    current = apply_operator(previous.astype(jnp.bfloat16), blocks_dev, global_ids)
    total = total + coeffs[1] * current
    for degree_step in range(2, DEG + 1):
        following = 2.0 * apply_operator(current.astype(jnp.bfloat16), blocks_dev, global_ids) - previous
        total = total + coeffs[degree_step] * following
        previous, current = current, following
    return total
```

```python
import jax
import jax.numpy as jnp
from jax import lax
from jax.experimental import pallas as pl
from jax.experimental.pallas import tpu as pltpu
from jax.sharding import PartitionSpec as P

BLK = 128
NNZ = 3
PROBES = 32
DEG = 8
ROWS = 104
HS = 8
HR = 4
HALO = 2 * HS + 2 * HR
UNIT = 8
UNITS = ROWS // UNIT
F32 = jnp.float32
BF16 = jnp.bfloat16
MESH = pl.DeviceIdType.MESH
cat = jnp.concatenate


def kernel(probes_hbm, blocks_hbm, col, send_sub, send_reg, coeffs, out_hbm,
           probes, raw, weights, state, landing, outgoing, cheb, total,
           in_sem, out_sem, send_sem, recv_sem):
    region = lax.axis_index("region")
    sub = lax.axis_index("sub")
    n_region = lax.axis_size("region")
    n_sub = lax.axis_size("sub")
    links = (
        (0, HS, "sub", lax.rem(sub + 1, n_sub)),
        (HS, HS, "sub", lax.rem(sub + n_sub - 1, n_sub)),
        (2 * HS, HR, "region", lax.rem(region + 1, n_region)),
        (2 * HS + HR, HR, "region", lax.rem(region + n_region - 1, n_region)),
    )

    def load_rows(u):
        rows = pl.ds(u * UNIT, UNIT)
        return pltpu.make_async_copy(blocks_hbm.at[rows], raw.at[rows], in_sem.at[u])

    probes_copy = pltpu.make_async_copy(probes_hbm, probes, in_sem.at[UNITS])
    probes_copy.start()
    for u in range(UNITS):
        load_rows(u).start()
    barrier = pltpu.get_barrier_semaphore()
    for _, _, axis, target in links:
        pl.semaphore_signal(barrier, inc=1, device_id={axis: target}, device_id_type=MESH)

    def listed(slot):
        if slot < HS:
            row = send_sub[0, 1, slot]
        elif slot < 2 * HS:
            row = send_sub[0, 0, slot - HS]
        elif slot < 2 * HS + HR:
            row = send_reg[0, 1, slot - 2 * HS]
        else:
            row = send_reg[0, 0, slot - 2 * HS - HR]
        return jnp.maximum(row, 0)

    def halo_copy(step, link):
        first, count, axis, target = links[link]
        slots = pl.ds(first, count)
        return pltpu.make_async_remote_copy(
            src_ref=outgoing.at[step, slots],
            dst_ref=landing.at[step, slots],
            send_sem=send_sem.at[step, link],
            recv_sem=recv_sem.at[step, link],
            device_id={axis: target},
            device_id_type=MESH,
        )

    def take_halo(step):
        for link in range(4):
            halo_copy(step, link).wait_recv()
        now = lax.rem(step, 2)
        for slot in range(HALO):
            state[now, ROWS + slot] = landing[step, slot]

    probes_copy.wait()
    first_coeff = coeffs[0]
    for i in range(ROWS):
        block = probes[:, i * BLK:(i + 1) * BLK]
        state[0, i] = block
        wide = block.astype(F32)
        cheb[0, i] = wide
        cheb[1, i] = jnp.zeros_like(wide)
        total[:, i * BLK:(i + 1) * BLK] = first_coeff * wide
    for slot in range(HALO):
        outgoing[0, slot] = state[0, listed(slot)]
    pl.semaphore_wait(barrier, 4)
    for link in range(4):
        halo_copy(0, link).start()

    def transpose_unit(u, carry):
        load_rows(u).wait()
        for i in range(UNIT):
            for k in range(NNZ):
                weights[u * UNIT + i, k] = raw[u * UNIT + i, k].T
        return carry

    lax.fori_loop(0, UNITS, transpose_unit, 0)
    take_halo(0)

    zero = jnp.zeros((PROBES, BLK), BF16)

    def issue(now, rows, accs):
        taken = [[state[now, col[r, k]] for k in range(NNZ)] for r in rows]
        for tile in range(3):
            for m in range(2):
                r = rows[4 * m:4 * m + 4]
                v = taken[4 * m:4 * m + 4]
                if tile < 2:
                    a, b = 2 * tile, 2 * tile + 1
                    rhs = cat([cat([weights[r[a], k], weights[r[b], k]], 1) for k in range(2)], 0)
                else:
                    rhs = cat([cat([weights[r[a], 2], weights[r[a + 1], 2]], 1) for a in (0, 2)], 0)
                staged = tile % 2
                pltpu.matmul_push_rhs(rhs, staged, m)
                if tile < 2:
                    lhs = cat([cat([v[a][0], v[a][1]], 1), cat([v[b][0], v[b][1]], 1)], 0)
                    pltpu.matmul_acc_lhs(accs[m][tile], lhs, staged)
                else:
                    upper = cat([cat([v[0][2], zero], 1), cat([v[1][2], zero], 1)], 0)
                    lower = cat([cat([zero, v[2][2]], 1), cat([zero, v[3][2]], 1)], 0)
                    pltpu.matmul_acc_lhs(accs[m][0], upper, staged)
                    pltpu.matmul_acc_lhs(accs[m][1], lower)

    def products(accs):
        result = []
        for m in range(2):
            for half in range(2):
                both = pltpu.matmul_pop(accs[m][half])
                result.append(both[:PROBES, :BLK])
                result.append(both[PROBES:, BLK:])
        return result

    def run(*a):
        sets = (((a[0], a[1]), (a[2], a[3])), ((a[4], a[5]), (a[6], a[7])))

        def one_step(step, carry):
            now = lax.rem(step, 2)
            later = 1 - now
            scale = jnp.where(step == 0, 1.0, 2.0).astype(F32)
            coeff = coeffs[step + 1]

            def finish_listed(unit, accs):
                for i, product in enumerate(products(accs)):
                    slot = unit * UNIT + i
                    new = scale * product - cheb[later, listed(slot)]
                    outgoing[step + 1, slot] = new.astype(BF16)

            def finish(unit, accs):
                for i, product in enumerate(products(accs)):
                    row = unit * UNIT + i
                    columns = slice(row * BLK, (row + 1) * BLK)
                    new = scale * product - cheb[later, row]
                    cheb[later, row] = new
                    state[later, row] = new.astype(BF16)
                    total[:, columns] += coeff * new

            @pl.when(step < DEG - 1)
            def _():
                for unit in range(3):
                    issue(now, [listed(unit * UNIT + i) for i in range(UNIT)], sets[unit % 2])
                    if unit == 1:
                        finish_listed(0, sets[0])
                        halo_copy(step + 1, 0).start()
                    elif unit == 2:
                        finish_listed(1, sets[1])
                        halo_copy(step + 1, 1).start()
                finish_listed(2, sets[0])
                halo_copy(step + 1, 2).start()
                halo_copy(step + 1, 3).start()

            for unit in range(UNITS):
                issue(now, [unit * UNIT + i for i in range(UNIT)], sets[unit % 2])
                if unit:
                    finish(unit - 1, sets[(unit - 1) % 2])
            finish(UNITS - 1, sets[(UNITS - 1) % 2])

            @pl.when(step < DEG - 1)
            def _():
                take_halo(step + 1)

            return carry

        lax.fori_loop(0, DEG, one_step, 0)

    pl.run_scoped(run, *[pltpu.ACC(mxu_id=m)((2 * PROBES, 2 * BLK), F32) for m in (0, 0, 1, 1, 0, 0, 1, 1)])

    out_copy = pltpu.make_async_copy(total, out_hbm, out_sem)
    out_copy.start()

    def sent(step, carry):
        for link in range(4):
            halo_copy(step, link).wait_send()
        return carry

    lax.fori_loop(0, DEG, sent, 0)
    out_copy.wait()


def local(probes, blocks, col_slot, send_sub, send_reg, coeffs):
    anywhere = pl.BlockSpec(memory_space=pl.ANY)
    scalar = pl.BlockSpec(memory_space=pltpu.SMEM)
    width = ROWS * BLK
    return pl.pallas_call(
        kernel,
        out_shape=jax.ShapeDtypeStruct((PROBES, width), F32),
        in_specs=[anywhere, anywhere, scalar, scalar, scalar, scalar],
        out_specs=anywhere,
        scratch_shapes=[
            pltpu.VMEM((PROBES, width), BF16),
            pltpu.VMEM((ROWS, NNZ, BLK, BLK), BF16),
            pltpu.VMEM((ROWS, NNZ, BLK, BLK), BF16),
            pltpu.VMEM((2, ROWS + HALO, PROBES, BLK), BF16),
            pltpu.VMEM((DEG, HALO, PROBES, BLK), BF16),
            pltpu.VMEM((DEG, HALO, PROBES, BLK), BF16),
            pltpu.VMEM((2, ROWS, PROBES, BLK), F32),
            pltpu.VMEM((PROBES, width), F32),
            pltpu.SemaphoreType.DMA((UNITS + 1,)),
            pltpu.SemaphoreType.DMA,
            pltpu.SemaphoreType.DMA((DEG, 4)),
            pltpu.SemaphoreType.DMA((DEG, 4)),
        ],
        compiler_params=pltpu.CompilerParams(
            collective_id=0, has_side_effects=True, vmem_limit_bytes=56 << 20
        ),
    )(probes, blocks, col_slot, send_sub, send_reg, coeffs)


def solution(mesh):
    both = ("region", "sub")
    mapped = jax.shard_map(
        local,
        mesh=mesh,
        in_specs=(
            P(None, both),
            P(both, None, None, None),
            P(both, None),
            P(both, None, None),
            P(both, None, None),
            P(),
        ),
        out_specs=P(None, both),
        check_vma=False,
    )

    def run(*args):
        with jax.sharding.use_abstract_mesh(mesh.abstract_mesh):
            return mapped(*args)

    return run
```

```python
import jax
import jax.numpy as jnp
from jax import lax
from jax.experimental import pallas as pl
from jax.experimental.pallas import tpu as pltpu
from jax.sharding import PartitionSpec as P

BLK = 128
NNZ = 3
PROBES = 32
DEG = 8
ROWS = 104
HS = 8
HR = 4
HALO = 2 * HS + 2 * HR
UNIT = 8
Z_SIZE = 8
UNITS = ROWS // UNIT
F32 = jnp.float32
BF16 = jnp.bfloat16
MESH = pl.DeviceIdType.MESH
cat = jnp.concatenate


def kernel(probes_hbm, blocks_hbm, col, send_sub, send_reg, coeffs, total,
           probes, raw, weights, state, landing, outgoing, cheb,
           in_sem, send_sem, recv_sem):
    region = lax.axis_index("region")
    sub = lax.axis_index("sub")
    last_region = lax.axis_size("region") - 1
    last_sub = lax.axis_size("sub") - 1
    links = (
        (0, HS, "sub", sub + 1, sub < last_sub, sub > 0),
        (HS, HS, "sub", sub - 1, sub > 0, sub < last_sub),
        (2 * HS, HR, "region", region + 1, region < last_region, region > 0),
        (2 * HS + HR, HR, "region", region - 1, region > 0, region < last_region),
    )
    urgent = jnp.where(lax.rem(sub, Z_SIZE) == 0, 1, 0)

    def load_rows(u):
        rows = pl.ds(u * UNIT, UNIT)
        return pltpu.make_async_copy(blocks_hbm.at[rows], raw.at[rows], in_sem.at[u])

    probes_copy = pltpu.make_async_copy(probes_hbm, probes, in_sem.at[UNITS])
    probes_copy.start()
    barrier = pltpu.get_barrier_semaphore()
    for _, _, axis, target, sends, _ in links:
        @pl.when(sends)
        def _():
            pl.semaphore_signal(barrier, inc=1, device_id={axis: target}, device_id_type=MESH)
    for u in range(UNITS):
        load_rows(u).start()

    def sub_list(which):
        return [(HS * which + i, jnp.maximum(send_sub[0, 1 - which, i], 0)) for i in range(HS)]

    first_list = sub_list(urgent)
    second_list = sub_list(1 - urgent)
    third_list = [
        (2 * HS + HR * which + i, jnp.maximum(send_reg[0, 1 - which, i], 0)) for which in range(2) for i in range(HR)
    ]

    def halo_copy(step, link):
        first, count, axis, target, _, _ = links[link]
        slots = pl.ds(first, count)
        return pltpu.make_async_remote_copy(
            src_ref=outgoing.at[step, slots],
            dst_ref=landing.at[step, slots],
            send_sem=send_sem.at[step, link],
            recv_sem=recv_sem.at[step, link],
            device_id={axis: target},
            device_id_type=MESH,
        )

    def send(step, link, when=True):
        @pl.when(jnp.logical_and(links[link][4], when))
        def _():
            halo_copy(step, link).start()

    def take_halo(step):
        now = lax.rem(step, 2)
        for link, (first, count, _, _, _, arrives) in enumerate(links):
            @pl.when(arrives)
            def _():
                halo_copy(step, link).wait_recv()
                for slot in range(first, first + count):
                    state[now, ROWS + slot] = landing[step, slot]

    probes_copy.wait()
    for i in range(ROWS):
        state[0, i] = probes[:, i * BLK:(i + 1) * BLK]
    zero = jnp.zeros((PROBES, BLK), BF16)
    for slot in range(HALO):
        for now in range(2):
            state[now, ROWS + slot] = zero
    for slot, row in first_list + second_list + third_list:
        outgoing[0, slot] = state[0, row]
    peers = sum(jnp.where(sends, 1, 0) for _, _, _, _, sends, _ in links)
    pl.semaphore_wait(barrier, peers)
    for link in range(4):
        send(0, link)
    first_coeff = coeffs[0]
    for i in range(ROWS):
        wide = probes[:, i * BLK:(i + 1) * BLK].astype(F32)
        cheb[0, i] = wide
        cheb[1, i] = jnp.zeros_like(wide)
        total[:, i * BLK:(i + 1) * BLK] = first_coeff * wide

    def transpose_unit(u, carry):
        load_rows(u).wait()
        for i in range(UNIT):
            for k in range(NNZ):
                weights[u * UNIT + i, k] = raw[u * UNIT + i, k].T
        return carry

    lax.fori_loop(0, UNITS, transpose_unit, 0)

    def push_own(rows, m, staged):
        r = rows[4 * m:4 * m + 4]
        rhs = cat([cat([weights[r[a], 0], weights[r[a + 1], 0]], 1) for a in (0, 2)], 0)
        pltpu.matmul_push_rhs(rhs, staged, m)

    def push_others(rows, m, pair):
        a, b = rows[4 * m + 2 * pair:4 * m + 2 * pair + 2]
        rhs = cat([cat([weights[a, k], weights[b, k]], 1) for k in (1, 2)], 0)
        pltpu.matmul_push_rhs(rhs, pair, m)

    def multiply_own(now, rows, m, accs, staged):
        v = [state[now, row] for row in rows[4 * m:4 * m + 4]]
        pltpu.matmul_acc_lhs(accs[m][0], cat([cat([v[0], zero], 1), cat([v[1], zero], 1)], 0), staged)
        pltpu.matmul_acc_lhs(accs[m][1], cat([cat([zero, v[2]], 1), cat([zero, v[3]], 1)], 0))

    def multiply_others(now, rows, m, pair, accs):
        lhs = [cat([state[now, col[k, row]] for k in (1, 2)], 1) for row in rows[4 * m + 2 * pair:4 * m + 2 * pair + 2]]
        pltpu.matmul_acc_lhs(accs[m][pair], cat(lhs, 0), pair)

    def issue_others(now, rows, accs):
        for pair in range(2):
            for m in range(2):
                push_others(rows, m, pair)
                multiply_others(now, rows, m, pair, accs)

    def issue_own(now, rows, accs, staged=0):
        for m in range(2):
            push_own(rows, m, staged)
            multiply_own(now, rows, m, accs, staged)

    def issue(now, rows, accs):
        for pair in range(2):
            for m in range(2):
                push_others(rows, m, pair)
                multiply_others(now, rows, m, pair, accs)
        issue_own(now, rows, accs)

    def products(accs):
        result = []
        for m in range(2):
            for half in range(2):
                both = pltpu.matmul_pop(accs[m][half])
                result.append(both[:PROBES, :BLK])
                result.append(both[PROBES:, BLK:])
        return result

    def unit_rows(unit):
        return [unit * UNIT + i for i in range(UNIT)]

    def run(*a):
        sets = (((a[0], a[1]), (a[2], a[3])), ((a[4], a[5]), (a[6], a[7])))

        def one_step(step, carry):
            now = lax.rem(step, 2)
            later = 1 - now
            scale = jnp.where(step == 0, 1.0, 2.0).astype(F32)
            coeff = coeffs[step + 1]

            def finish_list(slots, accs):
                for (slot, row), product in zip(slots, products(accs)):
                    outgoing[step + 1, slot] = (scale * product - cheb[later, row]).astype(BF16)

            def finish(unit, accs):
                for row, product in zip(unit_rows(unit), products(accs)):
                    new = scale * product - cheb[later, row]
                    cheb[later, row] = new
                    state[later, row] = new.astype(BF16)
                    total[:, row * BLK:(row + 1) * BLK] += coeff * new

            rows = [row for _, row in first_list]
            issue_own(now, rows, sets[0])
            for pair in range(2):
                for m in range(2):
                    push_others(rows, m, pair)
            take_halo(step)
            for pair in range(2):
                for m in range(2):
                    multiply_others(now, rows, m, pair, sets[0])
            finish_list(first_list, sets[0])
            send(step + 1, 0, urgent == 0)
            send(step + 1, 1, urgent == 1)
            issue(now, [row for _, row in second_list], sets[1])
            issue(now, [row for _, row in third_list], sets[0])
            finish_list(second_list, sets[1])
            send(step + 1, 0, urgent == 1)
            send(step + 1, 1, urgent == 0)
            for unit in range(UNITS):
                issue(now, unit_rows(unit), sets[(unit + 1) % 2])
                if unit:
                    finish(unit - 1, sets[unit % 2])
                else:
                    finish_list(third_list, sets[0])
                    send(step + 1, 2)
                    send(step + 1, 3)
            finish(UNITS - 1, sets[UNITS % 2])
            return carry

        lax.fori_loop(0, DEG - 1, one_step, 0)

        now = (DEG - 1) % 2
        coeff = coeffs[DEG]

        def finish_own(unit, accs):
            for row, product in zip(unit_rows(unit), products(accs)):
                total[:, row * BLK:(row + 1) * BLK] += coeff * (2.0 * product - cheb[1 - now, row])

        def finish_last(unit, accs):
            for row, product in zip(unit_rows(unit), products(accs)):
                total[:, row * BLK:(row + 1) * BLK] += coeff * (2.0 * product)

        for unit in range(UNITS):
            issue_own(now, unit_rows(unit), sets[unit % 2], unit % 2)
            if unit:
                finish_own(unit - 1, sets[(unit - 1) % 2])
        finish_own(UNITS - 1, sets[(UNITS - 1) % 2])
        take_halo(DEG - 1)
        for unit in range(UNITS):
            issue_others(now, unit_rows(unit), sets[unit % 2])
            if unit:
                finish_last(unit - 1, sets[(unit - 1) % 2])
        finish_last(UNITS - 1, sets[(UNITS - 1) % 2])

    pl.run_scoped(run, *[pltpu.ACC(mxu_id=m)((2 * PROBES, 2 * BLK), F32) for m in (0, 0, 1, 1, 0, 0, 1, 1)])

    def sent(step, carry):
        for link in range(4):
            @pl.when(links[link][4])
            def _():
                halo_copy(step, link).wait_send()
        return carry

    lax.fori_loop(0, DEG, sent, 0)


def local(probes, blocks, col_slot, send_sub, send_reg, coeffs):
    in_hbm = pl.BlockSpec(memory_space=pltpu.HBM)
    scalar = pl.BlockSpec(memory_space=pltpu.SMEM)
    width = ROWS * BLK
    args = (probes, blocks, col_slot.T, send_sub, send_reg, coeffs)
    return pl.pallas_call(
        kernel,
        out_shape=jax.ShapeDtypeStruct((PROBES, width), F32),
        in_specs=[in_hbm, in_hbm, scalar, scalar, scalar, scalar],
        out_specs=pl.BlockSpec(memory_space=pltpu.VMEM),
        scratch_shapes=[
            pltpu.VMEM((PROBES, width), BF16),
            pltpu.VMEM((ROWS, NNZ, BLK, BLK), BF16),
            pltpu.VMEM((ROWS, NNZ, BLK, BLK), BF16),
            pltpu.VMEM((2, ROWS + HALO, PROBES, BLK), BF16),
            pltpu.VMEM((DEG, HALO, PROBES, BLK), BF16),
            pltpu.VMEM((DEG, HALO, PROBES, BLK), BF16),
            pltpu.VMEM((2, ROWS, PROBES, BLK), F32),
            pltpu.SemaphoreType.DMA((UNITS + 1,)),
            pltpu.SemaphoreType.DMA((DEG, 4)),
            pltpu.SemaphoreType.DMA((DEG, 4)),
        ],
        compiler_params=pltpu.CompilerParams(
            collective_id=0, has_side_effects=True, vmem_limit_bytes=40 << 20
        ),
    )(*(pltpu.with_memory_space_constraint(x, pltpu.HBM) for x in args))


def solution(mesh):
    both = ("region", "sub")
    mapped = jax.shard_map(
        local,
        mesh=mesh,
        in_specs=(
            P(None, both),
            P(both, None, None, None),
            P(both, None),
            P(both, None, None),
            P(both, None, None),
            P(),
        ),
        out_specs=P(None, both),
        check_vma=False,
    )

    def run(*args):
        with jax.sharding.use_abstract_mesh(mesh.abstract_mesh):
            return mapped(*args)

    return run
```

```python
import jax
import jax.numpy as jnp
from jax import lax
from jax.experimental import pallas as pl
from jax.experimental.pallas import tpu as pltpu
from jax.sharding import PartitionSpec as P

BLK = 128
NNZ = 3
PROBES = 32
DEG = 8
ROWS = 104
HS = 8
HR = 4
HALO = 2 * HS + 2 * HR
UNIT = 8
Z_SIZE = 8
UNITS = ROWS // UNIT
F32 = jnp.float32
BF16 = jnp.bfloat16
MESH = pl.DeviceIdType.MESH
cat = jnp.concatenate


def kernel(probes_hbm, blocks_hbm, col_hbm, sub_hbm, reg_hbm, coeffs_hbm, total,
           probes, raw, weights, state, landing, outgoing, cheb,
           col, send_sub, send_reg, coeffs, in_sem, table_sem, send_sem, recv_sem):
    region = lax.axis_index("region")
    sub = lax.axis_index("sub")
    last_region = lax.axis_size("region") - 1
    last_sub = lax.axis_size("sub") - 1
    links = (
        (0, HS, "sub", sub + 1, sub < last_sub, sub > 0),
        (HS, HS, "sub", sub - 1, sub > 0, sub < last_sub),
        (2 * HS, HR, "region", region + 1, region < last_region, region > 0),
        (2 * HS + HR, HR, "region", region - 1, region > 0, region < last_region),
    )
    urgent = jnp.where(lax.rem(sub, Z_SIZE) == 0, 1, 0)

    def load_rows(u):
        rows = pl.ds(u * UNIT, UNIT)
        return pltpu.make_async_copy(blocks_hbm.at[rows], raw.at[rows], in_sem.at[u])

    barrier = pltpu.get_barrier_semaphore()
    for _, _, axis, target, sends, _ in links:
        @pl.when(sends)
        def _():
            pl.semaphore_signal(barrier, inc=1, device_id={axis: target}, device_id_type=MESH)
    probes_copy = pltpu.make_async_copy(probes_hbm, probes, in_sem.at[UNITS])
    probes_copy.start()
    tables = ((sub_hbm, send_sub), (reg_hbm, send_reg), (col_hbm, col), (coeffs_hbm, coeffs))
    table_copies = [pltpu.make_async_copy(src, dst, table_sem.at[i]) for i, (src, dst) in enumerate(tables)]
    for copy in table_copies:
        copy.start()
    table_copies[0].wait()
    table_copies[1].wait()

    def sub_list(which):
        return [(HS * which + i, jnp.maximum(send_sub[0, 1 - which, i], 0)) for i in range(HS)]

    first_list = sub_list(urgent)
    second_list = sub_list(1 - urgent)
    third_list = [
        (2 * HS + HR * which + i, jnp.maximum(send_reg[0, 1 - which, i], 0)) for which in range(2) for i in range(HR)
    ]

    def halo_copy(step, link):
        first, count, axis, target, _, _ = links[link]
        slots = pl.ds(first, count)
        return pltpu.make_async_remote_copy(
            src_ref=outgoing.at[step, slots],
            dst_ref=landing.at[step, slots],
            send_sem=send_sem.at[step, link],
            recv_sem=recv_sem.at[step, link],
            device_id={axis: target},
            device_id_type=MESH,
        )

    def send(step, link, when=True):
        @pl.when(jnp.logical_and(links[link][4], when))
        def _():
            halo_copy(step, link).start()

    def send_sub_link(step, which):
        send(step, 0, which == 0)
        send(step, 1, which == 1)

    def take_link(step, link, when=True):
        first, count, _, _, _, arrives = links[link]

        @pl.when(jnp.logical_and(arrives, when))
        def _():
            halo_copy(step, link).wait_recv()
            for slot in range(first, first + count):
                state[lax.rem(step, 2), ROWS + slot] = landing[step, slot]

    def take_halo(step):
        take_link(step, 2)
        take_link(step, 3)
        take_link(step, 0, urgent == 0)
        take_link(step, 1)
        take_link(step, 0, urgent == 1)

    zero = jnp.zeros((PROBES, BLK), BF16)
    for slot in range(HALO):
        for now in range(2):
            state[now, ROWS + slot] = zero
    probes_copy.wait()
    for u in range(UNITS):
        load_rows(u).start()
    for i in range(ROWS):
        state[0, i] = probes[:, i * BLK:(i + 1) * BLK]
    peers = sum(jnp.where(sends, 1, 0) for _, _, _, _, sends, _ in links)
    for slot, row in first_list + second_list + third_list:
        outgoing[0, slot] = state[0, row]
    pl.semaphore_wait(barrier, peers)
    send_sub_link(0, urgent)
    send_sub_link(0, 1 - urgent)
    send(0, 2)
    send(0, 3)
    table_copies[2].wait()
    table_copies[3].wait()
    first_coeff = coeffs[0]
    for i in range(ROWS):
        wide = probes[:, i * BLK:(i + 1) * BLK].astype(F32)
        cheb[0, i] = wide
        cheb[1, i] = jnp.zeros_like(wide)
        total[:, i * BLK:(i + 1) * BLK] = first_coeff * wide

    def transpose_unit(u, carry):
        load_rows(u).wait()
        for i in range(UNIT):
            for k in range(NNZ):
                weights[u * UNIT + i, k] = raw[u * UNIT + i, k].T
        return carry

    lax.fori_loop(0, UNITS, transpose_unit, 0)

    def push_own(rows, m, staged):
        r = rows[4 * m:4 * m + 4]
        rhs = cat([cat([weights[r[a], 0], weights[r[a + 1], 0]], 1) for a in (0, 2)], 0)
        pltpu.matmul_push_rhs(rhs, staged, m)

    def push_others(rows, m, pair):
        a, b = rows[4 * m + 2 * pair:4 * m + 2 * pair + 2]
        rhs = cat([cat([weights[a, k], weights[b, k]], 1) for k in (1, 2)], 0)
        pltpu.matmul_push_rhs(rhs, pair, m)

    def multiply_own(now, rows, m, accs, staged):
        v = [state[now, row] for row in rows[4 * m:4 * m + 4]]
        pltpu.matmul_acc_lhs(accs[m][0], cat([cat([v[0], zero], 1), cat([v[1], zero], 1)], 0), staged)
        pltpu.matmul_acc_lhs(accs[m][1], cat([cat([zero, v[2]], 1), cat([zero, v[3]], 1)], 0))

    def columns(rows):
        return [(col[1, row], col[2, row]) for row in rows]

    def multiply_others(now, taken, m, pair, accs):
        lhs = [cat([state[now, c] for c in both], 1) for both in taken[4 * m + 2 * pair:4 * m + 2 * pair + 2]]
        pltpu.matmul_acc_lhs(accs[m][pair], cat(lhs, 0), pair)

    def issue_others(now, rows, accs):
        taken = columns(rows)
        for pair in range(2):
            for m in range(2):
                push_others(rows, m, pair)
                multiply_others(now, taken, m, pair, accs)

    def issue_own(now, rows, accs, staged=0):
        for m in range(2):
            push_own(rows, m, staged)
            multiply_own(now, rows, m, accs, staged)

    def stage_others(rows):
        for pair in range(2):
            for m in range(2):
                push_others(rows, m, pair)

    def multiply_staged(now, taken, accs):
        for pair in range(2):
            for m in range(2):
                multiply_others(now, taken, m, pair, accs)

    def issue(now, rows, accs):
        issue_others(now, rows, accs)
        issue_own(now, rows, accs)

    def products(accs):
        result = []
        for m in range(2):
            for half in range(2):
                both = pltpu.matmul_pop(accs[m][half])
                result.append(both[:PROBES, :BLK])
                result.append(both[PROBES:, BLK:])
        return result

    def unit_rows(unit):
        return [unit * UNIT + i for i in range(UNIT)]

    def run(*a):
        sets = (((a[0], a[1]), (a[2], a[3])), ((a[4], a[5]), (a[6], a[7])))

        def one_step(step, carry):
            now = lax.rem(step, 2)
            later = 1 - now
            scale = jnp.where(step == 0, 1.0, 2.0).astype(F32)
            coeff = coeffs[step + 1]

            def finish_list(slots, accs):
                for (slot, row), product in zip(slots, products(accs)):
                    outgoing[step + 1, slot] = (scale * product - cheb[later, row]).astype(BF16)

            def finish(unit, accs):
                for row, product in zip(unit_rows(unit), products(accs)):
                    new = scale * product - cheb[later, row]
                    cheb[later, row] = new
                    state[later, row] = new.astype(BF16)
                    total[:, row * BLK:(row + 1) * BLK] += coeff * new

            rows = [row for _, row in first_list]
            issue_own(now, rows, sets[0])
            stage_others(rows)
            taken = columns(rows)
            take_halo(step)
            multiply_staged(now, taken, sets[0])
            finish_list(first_list, sets[0])
            send_sub_link(step + 1, urgent)
            issue(now, [row for _, row in second_list], sets[1])
            issue(now, [row for _, row in third_list], sets[0])
            finish_list(second_list, sets[1])
            send_sub_link(step + 1, 1 - urgent)
            for unit in range(UNITS):
                issue(now, unit_rows(unit), sets[(unit + 1) % 2])
                if unit:
                    finish(unit - 1, sets[unit % 2])
                else:
                    finish_list(third_list, sets[0])
                    send(step + 1, 2)
                    send(step + 1, 3)
            finish(UNITS - 1, sets[UNITS % 2])
            return carry

        lax.fori_loop(0, DEG - 1, one_step, 0)

        now = (DEG - 1) % 2
        coeff = coeffs[DEG]

        def finish_own(unit, accs):
            for row, product in zip(unit_rows(unit), products(accs)):
                total[:, row * BLK:(row + 1) * BLK] += coeff * (2.0 * product - cheb[1 - now, row])

        def finish_last(unit, accs):
            for row, product in zip(unit_rows(unit), products(accs)):
                total[:, row * BLK:(row + 1) * BLK] += coeff * (2.0 * product)

        for unit in range(UNITS):
            issue_own(now, unit_rows(unit), sets[unit % 2], unit % 2)
            if unit:
                finish_own(unit - 1, sets[(unit - 1) % 2])
        finish_own(UNITS - 1, sets[(UNITS - 1) % 2])
        stage_others(unit_rows(0))
        taken = columns(unit_rows(0))
        take_halo(DEG - 1)
        multiply_staged(now, taken, sets[0])
        for unit in range(UNITS):
            if unit:
                issue_others(now, unit_rows(unit), sets[unit % 2])
                finish_last(unit - 1, sets[(unit - 1) % 2])
        finish_last(UNITS - 1, sets[(UNITS - 1) % 2])

    pl.run_scoped(run, *[pltpu.ACC(mxu_id=m)((2 * PROBES, 2 * BLK), F32) for m in (0, 0, 1, 1, 0, 0, 1, 1)])

    def sent(step, carry):
        for link in range(4):
            @pl.when(links[link][4])
            def _():
                halo_copy(step, link).wait_send()
        return carry

    lax.fori_loop(0, DEG, sent, 0)


def local(probes, blocks, col_slot, send_sub, send_reg, coeffs):
    in_hbm = pl.BlockSpec(memory_space=pltpu.HBM)
    width = ROWS * BLK
    args = (probes, blocks, col_slot.T, send_sub, send_reg, coeffs)
    return pl.pallas_call(
        kernel,
        out_shape=jax.ShapeDtypeStruct((PROBES, width), F32),
        in_specs=[in_hbm] * 6,
        out_specs=pl.BlockSpec(memory_space=pltpu.VMEM),
        scratch_shapes=[
            pltpu.VMEM((PROBES, width), BF16),
            pltpu.VMEM((ROWS, NNZ, BLK, BLK), BF16),
            pltpu.VMEM((ROWS, NNZ, BLK, BLK), BF16),
            pltpu.VMEM((2, ROWS + HALO, PROBES, BLK), BF16),
            pltpu.VMEM((DEG, HALO, PROBES, BLK), BF16),
            pltpu.VMEM((DEG, HALO, PROBES, BLK), BF16),
            pltpu.VMEM((2, ROWS, PROBES, BLK), F32),
            pltpu.SMEM((NNZ, ROWS), jnp.int32),
            pltpu.SMEM((1, 2, HS), jnp.int32),
            pltpu.SMEM((1, 2, HR), jnp.int32),
            pltpu.SMEM((DEG + 1,), F32),
            pltpu.SemaphoreType.DMA((UNITS + 1,)),
            pltpu.SemaphoreType.DMA((4,)),
            pltpu.SemaphoreType.DMA((DEG, 4)),
            pltpu.SemaphoreType.DMA((DEG, 4)),
        ],
        compiler_params=pltpu.CompilerParams(
            collective_id=0, has_side_effects=True, vmem_limit_bytes=40 << 20
        ),
    )(*(pltpu.with_memory_space_constraint(x, pltpu.HBM) for x in args))


def solution(mesh):
    both = ("region", "sub")
    mapped = jax.shard_map(
        local,
        mesh=mesh,
        in_specs=(
            P(None, both),
            P(both, None, None, None),
            P(both, None),
            P(both, None, None),
            P(both, None, None),
            P(),
        ),
        out_specs=P(None, both),
        check_vma=False,
    )

    def run(*args):
        with jax.sharding.use_abstract_mesh(mesh.abstract_mesh):
            return mapped(*args)

    return run
```

```python
import jax
import jax.numpy as jnp
from jax import lax
from jax.experimental import pallas as pl
from jax.experimental.pallas import tpu as pltpu
from jax.sharding import PartitionSpec as P

BLK = 128
NNZ = 3
PROBES = 32
DEG = 8
ROWS = 104
HS = 8
HR = 4
HALO = 2 * HS + 2 * HR
UNIT = 8
Z_SIZE = 8
GROUPS = 2
PART = PROBES // GROUPS
UNITS = ROWS // UNIT
F32 = jnp.float32
BF16 = jnp.bfloat16
MESH = pl.DeviceIdType.MESH
cat = jnp.concatenate


def kernel(probes_hbm, blocks_hbm, col_hbm, sub_hbm, reg_hbm, coeffs_hbm, total,
           probes, raw, weights, state, land_sub, land_reg, out_sub, out_reg, cheb,
           col, send_sub, send_reg, coeffs, in_sem, table_sem, send_sem, recv_sem):
    region = lax.axis_index("region")
    sub = lax.axis_index("sub")
    last_region = lax.axis_size("region") - 1
    last_sub = lax.axis_size("sub") - 1
    links = (
        (0, HS, "sub", sub + 1, sub < last_sub, sub > 0),
        (HS, HS, "sub", sub - 1, sub > 0, sub < last_sub),
        (2 * HS, HR, "region", region + 1, region < last_region, region > 0),
        (2 * HS + HR, HR, "region", region - 1, region > 0, region < last_region),
    )
    urgent = jnp.where(lax.rem(sub, Z_SIZE) == 0, 1, 0)

    def load_rows(u):
        rows = pl.ds(u * UNIT, UNIT)
        return pltpu.make_async_copy(blocks_hbm.at[rows], raw.at[rows], in_sem.at[u])

    barrier = pltpu.get_barrier_semaphore()
    for _, _, axis, target, sends, _ in links:
        @pl.when(sends)
        def _():
            pl.semaphore_signal(barrier, inc=1, device_id={axis: target}, device_id_type=MESH)
    probes_copy = pltpu.make_async_copy(probes_hbm, probes, in_sem.at[UNITS])
    probes_copy.start()
    tables = ((sub_hbm, send_sub), (reg_hbm, send_reg), (col_hbm, col), (coeffs_hbm, coeffs))
    table_copies = [pltpu.make_async_copy(src, dst, table_sem.at[i]) for i, (src, dst) in enumerate(tables)]
    for copy in table_copies:
        copy.start()
    table_copies[0].wait()
    table_copies[1].wait()

    def sub_list(which):
        return [(HS * which + i, jnp.maximum(send_sub[0, 1 - which, i], 0)) for i in range(HS)]

    first_list = sub_list(urgent)
    second_list = sub_list(1 - urgent)
    third_list = [(HR * which + i, jnp.maximum(send_reg[0, 1 - which, i], 0)) for which in range(2) for i in range(HR)]

    def message(step, link, group=0):
        first, count, axis, target, _, _ = links[link]
        if link < 2:
            slots = pl.ds(first, count)
            src, dst, which = out_sub.at[step, group, slots], land_sub.at[step, group, slots], GROUPS * link + group
        else:
            slots = pl.ds(first - 2 * HS, count)
            src, dst, which = out_reg.at[step, slots], land_reg.at[step, slots], 2 * GROUPS + link - 2
        return pltpu.make_async_remote_copy(
            src_ref=src,
            dst_ref=dst,
            send_sem=send_sem.at[step, which],
            recv_sem=recv_sem.at[step, which],
            device_id={axis: target},
            device_id_type=MESH,
        )

    def send_reg_links(step):
        for link in (2, 3):
            @pl.when(links[link][4])
            def _():
                message(step, link).start()

    def send_sub_link(step, which, group):
        for link in range(2):
            @pl.when(jnp.logical_and(links[link][4], which == link))
            def _():
                message(step, link, group).start()

    def take_reg_links(step):
        for link in (2, 3):
            first, count, _, _, _, arrives = links[link]

            @pl.when(arrives)
            def _():
                message(step, link).wait_recv()
                for slot in range(first, first + count):
                    state[lax.rem(step, 2), ROWS + slot] = land_reg[step, slot - 2 * HS]

    def take_sub_link(step, which, group):
        for link in range(2):
            first, count, _, _, _, arrives = links[link]

            @pl.when(jnp.logical_and(arrives, which == link))
            def _():
                message(step, link, group).wait_recv()
                for slot in range(first, first + count):
                    state[lax.rem(step, 2), ROWS + slot, part(group)] = land_sub[step, group, slot]

    def part(group):
        return slice(group * PART, (group + 1) * PART)

    def take_early(step):
        take_reg_links(step)
        for group in range(GROUPS):
            take_sub_link(step, urgent, group)

    zero = jnp.zeros((PROBES, BLK), BF16)
    for slot in range(HALO):
        for now in range(2):
            state[now, ROWS + slot] = zero
    probes_copy.wait()
    for u in range(UNITS):
        load_rows(u).start()
    for i in range(ROWS):
        state[0, i] = probes[:, i * BLK:(i + 1) * BLK]
    peers = sum(jnp.where(sends, 1, 0) for _, _, _, _, sends, _ in links)
    for slot, row in first_list + second_list:
        for group in range(GROUPS):
            out_sub[0, group, slot] = state[0, row, part(group)]
    for slot, row in third_list:
        out_reg[0, slot] = state[0, row]
    pl.semaphore_wait(barrier, peers)
    for which in (urgent, 1 - urgent):
        for group in range(GROUPS):
            send_sub_link(0, which, group)
    send_reg_links(0)
    table_copies[2].wait()
    table_copies[3].wait()
    first_coeff = coeffs[0]
    for i in range(ROWS):
        wide = probes[:, i * BLK:(i + 1) * BLK].astype(F32)
        cheb[0, i] = wide
        cheb[1, i] = jnp.zeros_like(wide)
        total[:, i * BLK:(i + 1) * BLK] = first_coeff * wide

    def transpose_unit(u, carry):
        load_rows(u).wait()
        for i in range(UNIT):
            for k in range(NNZ):
                weights[u * UNIT + i, k] = raw[u * UNIT + i, k].T
        return carry

    lax.fori_loop(0, UNITS, transpose_unit, 0)

    def push_own(rows, m, staged):
        r = rows[4 * m:4 * m + 4]
        rhs = cat([cat([weights[r[a], 0], weights[r[a + 1], 0]], 1) for a in (0, 2)], 0)
        pltpu.matmul_push_rhs(rhs, staged, m)

    def push_others(rows, m, pair):
        a, b = rows[4 * m + 2 * pair:4 * m + 2 * pair + 2]
        rhs = cat([cat([weights[a, k], weights[b, k]], 1) for k in (1, 2)], 0)
        pltpu.matmul_push_rhs(rhs, pair, m)

    def multiply_own(now, rows, m, accs, staged):
        v = [state[now, row] for row in rows[4 * m:4 * m + 4]]
        pltpu.matmul_acc_lhs(accs[m][0], cat([cat([v[0], zero], 1), cat([v[1], zero], 1)], 0), staged)
        pltpu.matmul_acc_lhs(accs[m][1], cat([cat([zero, v[2]], 1), cat([zero, v[3]], 1)], 0))

    def columns(rows):
        return [(col[1, row], col[2, row]) for row in rows]

    def multiply_others(now, taken, m, pair, accs):
        lhs = [cat([state[now, c] for c in both], 1) for both in taken[4 * m + 2 * pair:4 * m + 2 * pair + 2]]
        pltpu.matmul_acc_lhs(accs[m][pair], cat(lhs, 0), pair)

    def issue_others(now, rows, accs):
        taken = columns(rows)
        for pair in range(2):
            for m in range(2):
                push_others(rows, m, pair)
                multiply_others(now, taken, m, pair, accs)

    def issue_own(now, rows, accs, staged=0):
        for m in range(2):
            push_own(rows, m, staged)
            multiply_own(now, rows, m, accs, staged)

    def stage_others(rows):
        for pair in range(2):
            for m in range(2):
                push_others(rows, m, pair)

    def multiply_staged(now, taken, accs):
        for pair in range(2):
            for m in range(2):
                multiply_others(now, taken, m, pair, accs)

    small_zero = jnp.zeros((PART, BLK), BF16)

    def issue_own_groups(now, rows, groups):
        for m in range(2):
            push_own(rows, m, 0)
            staged = 0
            for group in range(GROUPS):
                v = [state[now, row, part(group)] for row in rows[4 * m:4 * m + 4]]
                upper = cat([cat([v[0], small_zero], 1), cat([v[1], small_zero], 1)], 0)
                lower = cat([cat([small_zero, v[2]], 1), cat([small_zero, v[3]], 1)], 0)
                pltpu.matmul_acc_lhs(groups[group][m][0], upper, staged)
                pltpu.matmul_acc_lhs(groups[group][m][1], lower)
                staged = None

    def multiply_group(now, taken, group, accs):
        for pair in range(2):
            for m in range(2):
                lhs = [
                    cat([state[now, c, part(group)] for c in both], 1)
                    for both in taken[4 * m + 2 * pair:4 * m + 2 * pair + 2]
                ]
                pltpu.matmul_acc_lhs(accs[m][pair], cat(lhs, 0), pair)

    def issue(now, rows, accs):
        issue_others(now, rows, accs)
        issue_own(now, rows, accs)

    def products(accs, count=PROBES):
        result = []
        for m in range(2):
            for half in range(2):
                both = pltpu.matmul_pop(accs[m][half])
                result.append(both[:count, :BLK])
                result.append(both[count:, BLK:])
        return result

    def unit_rows(unit):
        return [unit * UNIT + i for i in range(UNIT)]

    def run(*a):
        quads = [((a[i], a[i + 1]), (a[i + 2], a[i + 3])) for i in range(0, len(a), 4)]
        sets, groups = quads[:2], quads[2:]

        def one_step(step, carry):
            now = lax.rem(step, 2)
            later = 1 - now
            scale = jnp.where(step == 0, 1.0, 2.0).astype(F32)
            coeff = coeffs[step + 1]

            def finish_urgent(group, accs):
                for (slot, row), product in zip(first_list, products(accs, PART)):
                    new = scale * product - cheb[later, row, part(group)]
                    out_sub[step + 1, group, slot] = new.astype(BF16)

            def finish_second(accs):
                for (slot, row), product in zip(second_list, products(accs)):
                    new = (scale * product - cheb[later, row]).astype(BF16)
                    for group in range(GROUPS):
                        out_sub[step + 1, group, slot] = new[part(group)]

            def finish_third(accs):
                for (slot, row), product in zip(third_list, products(accs)):
                    out_reg[step + 1, slot] = (scale * product - cheb[later, row]).astype(BF16)

            def finish(unit, accs):
                for row, product in zip(unit_rows(unit), products(accs)):
                    new = scale * product - cheb[later, row]
                    cheb[later, row] = new
                    state[later, row] = new.astype(BF16)
                    total[:, row * BLK:(row + 1) * BLK] += coeff * new

            rows = [row for _, row in first_list]
            issue_own_groups(now, rows, groups)
            stage_others(rows)
            taken = columns(rows)
            take_early(step)
            for group in range(GROUPS):
                take_sub_link(step, 1 - urgent, group)
                multiply_group(now, taken, group, groups[group])
                if group + 1 < GROUPS:
                    stage_others(rows)
                finish_urgent(group, groups[group])
                send_sub_link(step + 1, urgent, group)
            issue(now, [row for _, row in second_list], sets[1])
            issue(now, [row for _, row in third_list], sets[0])
            finish_second(sets[1])
            for group in range(GROUPS):
                send_sub_link(step + 1, 1 - urgent, group)
            for unit in range(UNITS):
                issue(now, unit_rows(unit), sets[(unit + 1) % 2])
                if unit:
                    finish(unit - 1, sets[unit % 2])
                else:
                    finish_third(sets[0])
                    send_reg_links(step + 1)
            finish(UNITS - 1, sets[UNITS % 2])
            return carry

        lax.fori_loop(0, DEG - 1, one_step, 0)

        now = (DEG - 1) % 2
        coeff = coeffs[DEG]

        def finish_own(unit, accs):
            for row, product in zip(unit_rows(unit), products(accs)):
                total[:, row * BLK:(row + 1) * BLK] += coeff * (2.0 * product - cheb[1 - now, row])

        def finish_last(unit, accs):
            for row, product in zip(unit_rows(unit), products(accs)):
                total[:, row * BLK:(row + 1) * BLK] += coeff * (2.0 * product)

        for unit in range(UNITS):
            issue_own(now, unit_rows(unit), sets[unit % 2], unit % 2)
            if unit:
                finish_own(unit - 1, sets[(unit - 1) % 2])
        finish_own(UNITS - 1, sets[(UNITS - 1) % 2])
        stage_others(unit_rows(0))
        taken = columns(unit_rows(0))
        take_early(DEG - 1)
        for group in range(GROUPS):
            take_sub_link(DEG - 1, 1 - urgent, group)
        multiply_staged(now, taken, sets[0])
        for unit in range(UNITS):
            if unit:
                issue_others(now, unit_rows(unit), sets[unit % 2])
                finish_last(unit - 1, sets[(unit - 1) % 2])
        finish_last(UNITS - 1, sets[(UNITS - 1) % 2])

    heights = (2 * PROBES,) * 2 + (2 * PART,) * GROUPS
    pl.run_scoped(run, *[pltpu.ACC(mxu_id=m)((height, 2 * BLK), F32) for height in heights for m in (0, 0, 1, 1)])

    def sent(step, carry):
        for link in range(4):
            for group in range(GROUPS if link < 2 else 1):
                @pl.when(links[link][4])
                def _():
                    message(step, link, group).wait_send()
        return carry

    lax.fori_loop(0, DEG, sent, 0)


def local(probes, blocks, col_slot, send_sub, send_reg, coeffs):
    in_hbm = pl.BlockSpec(memory_space=pltpu.HBM)
    width = ROWS * BLK
    args = (probes, blocks, col_slot.T, send_sub, send_reg, coeffs)
    return pl.pallas_call(
        kernel,
        out_shape=jax.ShapeDtypeStruct((PROBES, width), F32),
        in_specs=[in_hbm] * 6,
        out_specs=pl.BlockSpec(memory_space=pltpu.VMEM),
        scratch_shapes=[
            pltpu.VMEM((PROBES, width), BF16),
            pltpu.VMEM((ROWS, NNZ, BLK, BLK), BF16),
            pltpu.VMEM((ROWS, NNZ, BLK, BLK), BF16),
            pltpu.VMEM((2, ROWS + HALO, PROBES, BLK), BF16),
            pltpu.VMEM((DEG, GROUPS, 2 * HS, PART, BLK), BF16),
            pltpu.VMEM((DEG, 2 * HR, PROBES, BLK), BF16),
            pltpu.VMEM((DEG, GROUPS, 2 * HS, PART, BLK), BF16),
            pltpu.VMEM((DEG, 2 * HR, PROBES, BLK), BF16),
            pltpu.VMEM((2, ROWS, PROBES, BLK), F32),
            pltpu.SMEM((NNZ, ROWS), jnp.int32),
            pltpu.SMEM((1, 2, HS), jnp.int32),
            pltpu.SMEM((1, 2, HR), jnp.int32),
            pltpu.SMEM((DEG + 1,), F32),
            pltpu.SemaphoreType.DMA((UNITS + 1,)),
            pltpu.SemaphoreType.DMA((4,)),
            pltpu.SemaphoreType.DMA((DEG, 2 * GROUPS + 2)),
            pltpu.SemaphoreType.DMA((DEG, 2 * GROUPS + 2)),
        ],
        compiler_params=pltpu.CompilerParams(
            collective_id=0, has_side_effects=True, vmem_limit_bytes=40 << 20
        ),
    )(*(pltpu.with_memory_space_constraint(x, pltpu.HBM) for x in args))


def solution(mesh):
    both = ("region", "sub")
    mapped = jax.shard_map(
        local,
        mesh=mesh,
        in_specs=(
            P(None, both),
            P(both, None, None, None),
            P(both, None),
            P(both, None, None),
            P(both, None, None),
            P(),
        ),
        out_specs=P(None, both),
        check_vma=False,
    )

    def run(*args):
        with jax.sharding.use_abstract_mesh(mesh.abstract_mesh):
            return mapped(*args)

    return run
```

```python
import jax
import jax.numpy as jnp
from jax import lax
from jax.experimental import pallas as pl
from jax.experimental.pallas import tpu as pltpu
from jax.sharding import PartitionSpec as P

BLK = 128
NNZ = 3
PROBES = 32
DEG = 8
ROWS = 104
HS = 8
HR = 4
HALO = 2 * HS + 2 * HR
UNIT = 8
Z_SIZE = 8
GROUPS = 2
PART = PROBES // GROUPS
UNITS = ROWS // UNIT
F32 = jnp.float32
BF16 = jnp.bfloat16
MESH = pl.DeviceIdType.MESH
cat = jnp.concatenate


def kernel(probes_hbm, blocks_hbm, col_hbm, sub_hbm, reg_hbm, coeffs_hbm, total,
           probes, raw, weights, state, land_sub, land_reg, out_sub, out_reg, cheb,
           col, send_sub, send_reg, coeffs, in_sem, table_sem, send_sem, recv_sem):
    region = lax.axis_index("region")
    sub = lax.axis_index("sub")
    last_region = lax.axis_size("region") - 1
    last_sub = lax.axis_size("sub") - 1
    peers_at = (
        ("sub", sub + 1, sub < last_sub),
        ("sub", sub - 1, sub > 0),
        ("region", region + 1, region < last_region),
        ("region", region - 1, region > 0),
    )
    urgent = jnp.where(lax.rem(sub, Z_SIZE) == 0, 1, 0)

    def load_rows(u):
        rows = pl.ds(u * UNIT, UNIT)
        return pltpu.make_async_copy(blocks_hbm.at[rows], raw.at[rows], in_sem.at[u])

    barrier = pltpu.get_barrier_semaphore()
    for axis, target, there in peers_at:
        @pl.when(there)
        def _():
            pl.semaphore_signal(barrier, inc=1, device_id={axis: target}, device_id_type=MESH)
    probes_copy = pltpu.make_async_copy(probes_hbm, probes, in_sem.at[UNITS])
    probes_copy.start()
    tables = ((sub_hbm, send_sub), (reg_hbm, send_reg), (col_hbm, col), (coeffs_hbm, coeffs))
    table_copies = [pltpu.make_async_copy(src, dst, table_sem.at[i]) for i, (src, dst) in enumerate(tables)]
    for copy in table_copies:
        copy.start()
    for u in range(UNITS):
        load_rows(u).start()
    table_copies[0].wait()
    table_copies[1].wait()

    def sub_list(which):
        return [(HS * which + i, jnp.maximum(send_sub[0, 1 - which, i], 0)) for i in range(HS)]

    first_list = sub_list(urgent)
    second_list = sub_list(1 - urgent)
    third_list = [(HR * which + i, jnp.maximum(send_reg[0, 1 - which, i], 0)) for which in range(2) for i in range(HR)]

    def remote_copy(src, dst, step, which, axis, target):
        return pltpu.make_async_remote_copy(
            src_ref=src,
            dst_ref=dst,
            send_sem=send_sem.at[step, which],
            recv_sem=recv_sem.at[step, which],
            device_id={axis: target},
            device_id_type=MESH,
        )

    def sub_message(step, link, group):
        slots = pl.ds(HS * link, HS)
        target = sub + 1 - 2 * link
        return remote_copy(
            out_sub.at[step, group, slots], land_sub.at[step, group, slots], step, GROUPS * link + group, "sub", target
        )

    def reg_message(step, link):
        slots = pl.ds(HR * link, HR)
        target = region + 1 - 2 * link
        return remote_copy(out_reg.at[step, slots], land_reg.at[step, slots], step, 2 * GROUPS + link, "region", target)

    def has_target(link, place, last):
        return jnp.logical_or(jnp.logical_and(link == 0, place < last), jnp.logical_and(link == 1, place > 0))

    def send_reg_links(step):
        for link in range(2):
            @pl.when(has_target(link, region, last_region))
            def _():
                reg_message(step, link).start()

    def send_sub_link(step, link, group):
        @pl.when(has_target(link, sub, last_sub))
        def _():
            sub_message(step, link, group).start()

    def take_reg_links(step):
        for link in range(2):
            @pl.when(has_target(1 - link, region, last_region))
            def _():
                reg_message(step, link).wait_recv()
                for slot in range(HR * link, HR * (link + 1)):
                    state[lax.rem(step, 2), ROWS + 2 * HS + slot] = land_reg[step, slot]

    def take_sub_link(step, link, group):
        @pl.when(has_target(1 - link, sub, last_sub))
        def _():
            sub_message(step, link, group).wait_recv()
            for i in range(HS):
                slot = HS * link + i
                state[lax.rem(step, 2), ROWS + slot, part(group)] = land_sub[step, group, slot]

    def part(group):
        return slice(group * PART, (group + 1) * PART)

    def take_early(step):
        take_reg_links(step)
        for group in range(GROUPS):
            take_sub_link(step, urgent, group)

    zero = jnp.zeros((PROBES, BLK), BF16)
    for slot in range(HALO):
        for now in range(2):
            state[now, ROWS + slot] = zero
    probes_copy.wait()
    for i in range(ROWS):
        state[0, i] = probes[:, i * BLK:(i + 1) * BLK]
    peers = sum(jnp.where(there, 1, 0) for _, _, there in peers_at)
    for slot, row in first_list + second_list:
        for group in range(GROUPS):
            out_sub[0, group, slot] = state[0, row, part(group)]
    for slot, row in third_list:
        out_reg[0, slot] = state[0, row]
    pl.semaphore_wait(barrier, peers)
    for which in (urgent, 1 - urgent):
        for group in range(GROUPS):
            send_sub_link(0, which, group)
    send_reg_links(0)
    table_copies[2].wait()
    table_copies[3].wait()
    first_coeff = coeffs[0]
    for i in range(ROWS):
        wide = probes[:, i * BLK:(i + 1) * BLK].astype(F32)
        cheb[0, i] = wide
        cheb[1, i] = jnp.zeros_like(wide)
        total[:, i * BLK:(i + 1) * BLK] = first_coeff * wide

    def transpose_unit(u, carry):
        load_rows(u).wait()
        for i in range(UNIT):
            for k in range(NNZ):
                weights[u * UNIT + i, k] = raw[u * UNIT + i, k].T
        return carry

    lax.fori_loop(0, UNITS, transpose_unit, 0)

    def push_own(rows, m, staged):
        r = rows[4 * m:4 * m + 4]
        rhs = cat([cat([weights[r[a], 0], weights[r[a + 1], 0]], 1) for a in (0, 2)], 0)
        pltpu.matmul_push_rhs(rhs, staged, m)

    def push_others(rows, m, pair):
        a, b = rows[4 * m + 2 * pair:4 * m + 2 * pair + 2]
        rhs = cat([cat([weights[a, k], weights[b, k]], 1) for k in (1, 2)], 0)
        pltpu.matmul_push_rhs(rhs, pair, m)

    def multiply_own(now, rows, m, accs, staged):
        v = [state[now, row] for row in rows[4 * m:4 * m + 4]]
        pltpu.matmul_acc_lhs(accs[m][0], cat([cat([v[0], zero], 1), cat([v[1], zero], 1)], 0), staged)
        pltpu.matmul_acc_lhs(accs[m][1], cat([cat([zero, v[2]], 1), cat([zero, v[3]], 1)], 0))

    def columns(rows):
        return [(col[1, row], col[2, row]) for row in rows]

    def multiply_others(now, taken, m, pair, accs):
        lhs = [cat([state[now, c] for c in both], 1) for both in taken[4 * m + 2 * pair:4 * m + 2 * pair + 2]]
        pltpu.matmul_acc_lhs(accs[m][pair], cat(lhs, 0), pair)

    def issue_others(now, rows, accs):
        taken = columns(rows)
        for pair in range(2):
            for m in range(2):
                push_others(rows, m, pair)
                multiply_others(now, taken, m, pair, accs)

    def issue_own(now, rows, accs, staged=0):
        for m in range(2):
            push_own(rows, m, staged)
            multiply_own(now, rows, m, accs, staged)

    def stage_others(rows):
        for pair in range(2):
            for m in range(2):
                push_others(rows, m, pair)

    def multiply_staged(now, taken, accs):
        for pair in range(2):
            for m in range(2):
                multiply_others(now, taken, m, pair, accs)

    small_zero = jnp.zeros((PART, BLK), BF16)

    def issue_own_groups(now, rows, groups):
        for m in range(2):
            push_own(rows, m, 0)
            staged = 0
            for group in range(GROUPS):
                v = [state[now, row, part(group)] for row in rows[4 * m:4 * m + 4]]
                upper = cat([cat([v[0], small_zero], 1), cat([v[1], small_zero], 1)], 0)
                lower = cat([cat([small_zero, v[2]], 1), cat([small_zero, v[3]], 1)], 0)
                pltpu.matmul_acc_lhs(groups[group][m][0], upper, staged)
                pltpu.matmul_acc_lhs(groups[group][m][1], lower)
                staged = None

    def multiply_group(now, taken, group, accs):
        for pair in range(2):
            for m in range(2):
                lhs = [
                    cat([state[now, c, part(group)] for c in both], 1)
                    for both in taken[4 * m + 2 * pair:4 * m + 2 * pair + 2]
                ]
                pltpu.matmul_acc_lhs(accs[m][pair], cat(lhs, 0), pair)

    def issue(now, rows, accs):
        issue_others(now, rows, accs)
        issue_own(now, rows, accs)

    def products(accs, count=PROBES):
        result = []
        for m in range(2):
            for half in range(2):
                both = pltpu.matmul_pop(accs[m][half])
                result.append(both[:count, :BLK])
                result.append(both[count:, BLK:])
        return result

    def unit_rows(unit):
        return [unit * UNIT + i for i in range(UNIT)]

    def run(*a):
        quads = [((a[i], a[i + 1]), (a[i + 2], a[i + 3])) for i in range(0, len(a), 4)]
        sets, groups = quads[:2], quads[2:]

        def one_step(step, carry):
            now = lax.rem(step, 2)
            later = 1 - now
            scale = jnp.where(step == 0, 1.0, 2.0).astype(F32)
            coeff = coeffs[step + 1]

            def finish_urgent(group, accs):
                for (slot, row), product in zip(first_list, products(accs, PART)):
                    new = scale * product - cheb[later, row, part(group)]
                    out_sub[step + 1, group, slot] = new.astype(BF16)

            def finish_second(accs):
                for (slot, row), product in zip(second_list, products(accs)):
                    new = (scale * product - cheb[later, row]).astype(BF16)
                    for group in range(GROUPS):
                        out_sub[step + 1, group, slot] = new[part(group)]

            def finish_third(accs):
                for (slot, row), product in zip(third_list, products(accs)):
                    out_reg[step + 1, slot] = (scale * product - cheb[later, row]).astype(BF16)

            def finish(unit, accs):
                for row, product in zip(unit_rows(unit), products(accs)):
                    new = scale * product - cheb[later, row]
                    cheb[later, row] = new
                    state[later, row] = new.astype(BF16)
                    total[:, row * BLK:(row + 1) * BLK] += coeff * new

            rows = [row for _, row in first_list]
            issue_own_groups(now, rows, groups)
            stage_others(rows)
            taken = columns(rows)
            take_early(step)
            for group in range(GROUPS):
                take_sub_link(step, 1 - urgent, group)
                multiply_group(now, taken, group, groups[group])
                finish_urgent(group, groups[group])
                send_sub_link(step + 1, urgent, group)
                if group + 1 < GROUPS:
                    stage_others(rows)
            issue(now, [row for _, row in second_list], sets[1])
            issue(now, [row for _, row in third_list], sets[0])
            finish_second(sets[1])
            for group in range(GROUPS):
                send_sub_link(step + 1, 1 - urgent, group)
            for unit in range(UNITS):
                issue(now, unit_rows(unit), sets[(unit + 1) % 2])
                if unit:
                    finish(unit - 1, sets[unit % 2])
                else:
                    finish_third(sets[0])
                    send_reg_links(step + 1)
            finish(UNITS - 1, sets[UNITS % 2])
            return carry

        lax.fori_loop(0, DEG - 1, one_step, 0)

        now = (DEG - 1) % 2
        coeff = coeffs[DEG]

        def finish_own(unit, accs):
            for row, product in zip(unit_rows(unit), products(accs)):
                total[:, row * BLK:(row + 1) * BLK] += coeff * (2.0 * product - cheb[1 - now, row])

        def finish_last(unit, accs):
            for row, product in zip(unit_rows(unit), products(accs)):
                total[:, row * BLK:(row + 1) * BLK] += coeff * (2.0 * product)

        for unit in range(UNITS):
            issue_own(now, unit_rows(unit), sets[unit % 2], unit % 2)
            if unit:
                finish_own(unit - 1, sets[(unit - 1) % 2])
        finish_own(UNITS - 1, sets[(UNITS - 1) % 2])
        stage_others(unit_rows(0))
        taken = columns(unit_rows(0))
        take_early(DEG - 1)
        for group in range(GROUPS):
            take_sub_link(DEG - 1, 1 - urgent, group)
        multiply_staged(now, taken, sets[0])
        for unit in range(UNITS):
            if unit:
                issue_others(now, unit_rows(unit), sets[unit % 2])
                finish_last(unit - 1, sets[(unit - 1) % 2])
        finish_last(UNITS - 1, sets[(UNITS - 1) % 2])

    heights = (2 * PROBES,) * 2 + (2 * PART,) * GROUPS
    pl.run_scoped(run, *[pltpu.ACC(mxu_id=m)((height, 2 * BLK), F32) for height in heights for m in (0, 0, 1, 1)])

    def sent(step, carry):
        for link in range(2):
            @pl.when(has_target(link, sub, last_sub))
            def _():
                for group in range(GROUPS):
                    sub_message(step, link, group).wait_send()

            @pl.when(has_target(link, region, last_region))
            def _():
                reg_message(step, link).wait_send()
        return carry

    lax.fori_loop(0, DEG, sent, 0)


def local(probes, blocks, col_slot, send_sub, send_reg, coeffs):
    in_hbm = pl.BlockSpec(memory_space=pltpu.HBM)
    width = ROWS * BLK
    args = (probes, blocks, col_slot.T, send_sub, send_reg, coeffs)
    return pl.pallas_call(
        kernel,
        out_shape=jax.ShapeDtypeStruct((PROBES, width), F32),
        in_specs=[in_hbm] * 6,
        out_specs=pl.BlockSpec(memory_space=pltpu.VMEM),
        scratch_shapes=[
            pltpu.VMEM((PROBES, width), BF16),
            pltpu.VMEM((ROWS, NNZ, BLK, BLK), BF16),
            pltpu.VMEM((ROWS, NNZ, BLK, BLK), BF16),
            pltpu.VMEM((2, ROWS + HALO, PROBES, BLK), BF16),
            pltpu.VMEM((DEG, GROUPS, 2 * HS, PART, BLK), BF16),
            pltpu.VMEM((DEG, 2 * HR, PROBES, BLK), BF16),
            pltpu.VMEM((DEG, GROUPS, 2 * HS, PART, BLK), BF16),
            pltpu.VMEM((DEG, 2 * HR, PROBES, BLK), BF16),
            pltpu.VMEM((2, ROWS, PROBES, BLK), F32),
            pltpu.SMEM((NNZ, ROWS), jnp.int32),
            pltpu.SMEM((1, 2, HS), jnp.int32),
            pltpu.SMEM((1, 2, HR), jnp.int32),
            pltpu.SMEM((DEG + 1,), F32),
            pltpu.SemaphoreType.DMA((UNITS + 1,)),
            pltpu.SemaphoreType.DMA((4,)),
            pltpu.SemaphoreType.DMA((DEG, 2 * GROUPS + 2)),
            pltpu.SemaphoreType.DMA((DEG, 2 * GROUPS + 2)),
        ],
        compiler_params=pltpu.CompilerParams(
            collective_id=0, has_side_effects=True, vmem_limit_bytes=40 << 20
        ),
    )(*(pltpu.with_memory_space_constraint(x, pltpu.HBM) for x in args))


def solution(mesh):
    both = ("region", "sub")
    mapped = jax.shard_map(
        local,
        mesh=mesh,
        in_specs=(
            P(None, both),
            P(both, None, None, None),
            P(both, None),
            P(both, None, None),
            P(both, None, None),
            P(),
        ),
        out_specs=P(None, both),
        check_vma=False,
    )

    def run(*args):
        with jax.sharding.use_abstract_mesh(mesh.abstract_mesh):
            return mapped(*args)

    return run
```

```python
import jax
import jax.numpy as jnp
from jax import lax
from jax.experimental import pallas as pl
from jax.experimental.pallas import tpu as pltpu
from jax.sharding import PartitionSpec as P

BLK = 128
NNZ = 3
PROBES = 32
DEG = 8
ROWS = 104
HS = 8
HR = 4
HALO = 2 * HS + 2 * HR
UNIT = 8
Z_SIZE = 8
GROUPS = 2
PART = PROBES // GROUPS
UNITS = ROWS // UNIT
F32 = jnp.float32
BF16 = jnp.bfloat16
MESH = pl.DeviceIdType.MESH
cat = jnp.concatenate


def kernel(probes_hbm, blocks_hbm, col_hbm, sub_hbm, reg_hbm, coeffs_hbm, total,
           probes, raw, weights, state, land_sub, land_reg, out_sub, out_reg, cheb,
           col, send_sub, send_reg, coeffs, in_sem, table_sem, send_sem, recv_sem):
    region = lax.axis_index("region")
    sub = lax.axis_index("sub")
    last_region = lax.axis_size("region") - 1
    last_sub = lax.axis_size("sub") - 1
    peers_at = (
        ("sub", sub + 1, sub < last_sub),
        ("sub", sub - 1, sub > 0),
        ("region", region + 1, region < last_region),
        ("region", region - 1, region > 0),
    )
    urgent = jnp.where(lax.rem(sub, Z_SIZE) == 0, 1, 0)

    def load_rows(u):
        rows = pl.ds(u * UNIT, UNIT)
        return pltpu.make_async_copy(blocks_hbm.at[rows], raw.at[rows], in_sem.at[u])

    barrier = pltpu.get_barrier_semaphore()
    for axis, target, there in peers_at:
        @pl.when(there)
        def _():
            pl.semaphore_signal(barrier, inc=1, device_id={axis: target}, device_id_type=MESH)
    probes_copy = pltpu.make_async_copy(probes_hbm, probes, in_sem.at[UNITS])
    probes_copy.start()
    tables = ((sub_hbm, send_sub), (reg_hbm, send_reg), (col_hbm, col), (coeffs_hbm, coeffs))
    table_copies = [pltpu.make_async_copy(src, dst, table_sem.at[i]) for i, (src, dst) in enumerate(tables)]
    for copy in table_copies:
        copy.start()
    for u in range(UNITS):
        load_rows(u).start()
    table_copies[0].wait()
    table_copies[1].wait()

    def sub_list(which):
        return [(HS * which + i, jnp.maximum(send_sub[0, 1 - which, i], 0)) for i in range(HS)]

    first_list = sub_list(urgent)
    second_list = sub_list(1 - urgent)
    third_list = [(HR * which + i, jnp.maximum(send_reg[0, 1 - which, i], 0)) for which in range(2) for i in range(HR)]

    def remote_copy(src, dst, step, which, axis, target):
        return pltpu.make_async_remote_copy(
            src_ref=src,
            dst_ref=dst,
            send_sem=send_sem.at[step, which],
            recv_sem=recv_sem.at[step, which],
            device_id={axis: target},
            device_id_type=MESH,
        )

    def sub_message(step, link, group):
        slots = pl.ds(HS * link, HS)
        target = sub + 1 - 2 * link
        return remote_copy(
            out_sub.at[step, group, slots], land_sub.at[step, group, slots], step, GROUPS * link + group, "sub", target
        )

    def reg_message(step, link):
        slots = pl.ds(HR * link, HR)
        target = region + 1 - 2 * link
        return remote_copy(out_reg.at[step, slots], land_reg.at[step, slots], step, 2 * GROUPS + link, "region", target)

    def has_target(link, place, last):
        return jnp.logical_or(jnp.logical_and(link == 0, place < last), jnp.logical_and(link == 1, place > 0))

    def send_reg_links(step):
        for link in range(2):
            @pl.when(has_target(link, region, last_region))
            def _():
                reg_message(step, link).start()

    def send_sub_link(step, link, group):
        @pl.when(has_target(link, sub, last_sub))
        def _():
            sub_message(step, link, group).start()

    def take_reg_links(step):
        for link in range(2):
            @pl.when(has_target(1 - link, region, last_region))
            def _():
                reg_message(step, link).wait_recv()
                for slot in range(HR * link, HR * (link + 1)):
                    state[lax.rem(step, 2), ROWS + 2 * HS + slot] = land_reg[step, slot]

    def take_sub_link(step, link, group):
        @pl.when(has_target(1 - link, sub, last_sub))
        def _():
            sub_message(step, link, group).wait_recv()
            for i in range(HS):
                slot = HS * link + i
                state[lax.rem(step, 2), ROWS + slot, part(group)] = land_sub[step, group, slot]

    def part(group):
        return slice(group * PART, (group + 1) * PART)

    def take_early(step):
        take_reg_links(step)
        for group in range(GROUPS):
            take_sub_link(step, urgent, group)

    zero = jnp.zeros((PROBES, BLK), BF16)
    for slot in range(HALO):
        for now in range(2):
            state[now, ROWS + slot] = zero
    probes_copy.wait()
    for i in range(ROWS):
        state[0, i] = probes[:, i * BLK:(i + 1) * BLK]
    peers = sum(jnp.where(there, 1, 0) for _, _, there in peers_at)
    for slot, row in first_list + second_list:
        for group in range(GROUPS):
            out_sub[0, group, slot] = state[0, row, part(group)]
    for slot, row in third_list:
        out_reg[0, slot] = state[0, row]
    pl.semaphore_wait(barrier, peers)
    for which in (urgent, 1 - urgent):
        for group in range(GROUPS):
            send_sub_link(0, which, group)
    send_reg_links(0)
    table_copies[2].wait()
    table_copies[3].wait()
    first_coeff = coeffs[0]
    for i in range(ROWS):
        wide = probes[:, i * BLK:(i + 1) * BLK].astype(F32)
        cheb[0, i] = wide
        cheb[1, i] = jnp.zeros_like(wide)
        total[:, i * BLK:(i + 1) * BLK] = first_coeff * wide

    def transpose_unit(u, carry):
        load_rows(u).wait()
        for i in range(UNIT):
            for k in range(NNZ):
                weights[u * UNIT + i, k] = raw[u * UNIT + i, k].T
        return carry

    lax.fori_loop(0, UNITS, transpose_unit, 0)

    def push_own(rows, m, staged):
        r = rows[4 * m:4 * m + 4]
        rhs = cat([cat([weights[r[a], 0], weights[r[a + 1], 0]], 1) for a in (0, 2)], 0)
        pltpu.matmul_push_rhs(rhs, staged, m)

    def push_others(rows, m, pair):
        a, b = rows[4 * m + 2 * pair:4 * m + 2 * pair + 2]
        rhs = cat([cat([weights[a, k], weights[b, k]], 1) for k in (1, 2)], 0)
        pltpu.matmul_push_rhs(rhs, pair, m)

    def multiply_own(now, rows, m, accs, staged):
        v = [state[now, row] for row in rows[4 * m:4 * m + 4]]
        pltpu.matmul_acc_lhs(accs[m][0], cat([cat([v[0], zero], 1), cat([v[1], zero], 1)], 0), staged)
        pltpu.matmul_acc_lhs(accs[m][1], cat([cat([zero, v[2]], 1), cat([zero, v[3]], 1)], 0))

    def columns(rows):
        return [(col[1, row], col[2, row]) for row in rows]

    def multiply_others(now, taken, m, pair, accs):
        lhs = [cat([state[now, c] for c in both], 1) for both in taken[4 * m + 2 * pair:4 * m + 2 * pair + 2]]
        pltpu.matmul_acc_lhs(accs[m][pair], cat(lhs, 0), pair)

    def issue_others(now, rows, accs):
        taken = columns(rows)
        for pair in range(2):
            for m in range(2):
                push_others(rows, m, pair)
                multiply_others(now, taken, m, pair, accs)

    def issue_own(now, rows, accs, staged=0):
        for m in range(2):
            push_own(rows, m, staged)
            multiply_own(now, rows, m, accs, staged)

    def stage_others(rows):
        for pair in range(2):
            for m in range(2):
                push_others(rows, m, pair)

    def multiply_staged(now, taken, accs):
        for pair in range(2):
            for m in range(2):
                multiply_others(now, taken, m, pair, accs)

    small_zero = jnp.zeros((PART, BLK), BF16)

    def issue_own_groups(now, rows, groups):
        for m in range(2):
            push_own(rows, m, 0)
            staged = 0
            for group in range(GROUPS):
                v = [state[now, row, part(group)] for row in rows[4 * m:4 * m + 4]]
                upper = cat([cat([v[0], small_zero], 1), cat([v[1], small_zero], 1)], 0)
                lower = cat([cat([small_zero, v[2]], 1), cat([small_zero, v[3]], 1)], 0)
                pltpu.matmul_acc_lhs(groups[group][m][0], upper, staged)
                pltpu.matmul_acc_lhs(groups[group][m][1], lower)
                staged = None

    def multiply_group(now, taken, group, accs):
        for pair in range(2):
            for m in range(2):
                lhs = [
                    cat([state[now, c, part(group)] for c in both], 1)
                    for both in taken[4 * m + 2 * pair:4 * m + 2 * pair + 2]
                ]
                pltpu.matmul_acc_lhs(accs[m][pair], cat(lhs, 0), pair)

    def issue(now, rows, accs):
        issue_others(now, rows, accs)
        issue_own(now, rows, accs)

    def products(accs, count=PROBES):
        result = []
        for m in range(2):
            for half in range(2):
                both = pltpu.matmul_pop(accs[m][half])
                result.append(both[:count, :BLK])
                result.append(both[count:, BLK:])
        return result

    def unit_rows(unit):
        return [unit * UNIT + i for i in range(UNIT)]

    def sent(step, carry):
        for link in range(2):
            @pl.when(has_target(link, sub, last_sub))
            def _():
                for group in range(GROUPS):
                    sub_message(step, link, group).wait_send()

            @pl.when(has_target(link, region, last_region))
            def _():
                reg_message(step, link).wait_send()
        return carry

    def run(*a):
        quads = [((a[i], a[i + 1]), (a[i + 2], a[i + 3])) for i in range(0, len(a), 4)]
        sets, groups = quads[:2], quads[2:]

        def one_step(step, carry):
            now = lax.rem(step, 2)
            later = 1 - now
            scale = jnp.where(step == 0, 1.0, 2.0).astype(F32)
            coeff = coeffs[step + 1]

            def finish_urgent(group, accs):
                for (slot, row), product in zip(first_list, products(accs, PART)):
                    new = scale * product - cheb[later, row, part(group)]
                    out_sub[step + 1, group, slot] = new.astype(BF16)

            def finish_second(accs):
                for (slot, row), product in zip(second_list, products(accs)):
                    new = (scale * product - cheb[later, row]).astype(BF16)
                    for group in range(GROUPS):
                        out_sub[step + 1, group, slot] = new[part(group)]

            def finish_third(accs):
                for (slot, row), product in zip(third_list, products(accs)):
                    out_reg[step + 1, slot] = (scale * product - cheb[later, row]).astype(BF16)

            def finish(unit, accs):
                for row, product in zip(unit_rows(unit), products(accs)):
                    new = scale * product - cheb[later, row]
                    cheb[later, row] = new
                    state[later, row] = new.astype(BF16)
                    total[:, row * BLK:(row + 1) * BLK] += coeff * new

            rows = [row for _, row in first_list]
            issue_own_groups(now, rows, groups)
            stage_others(rows)
            taken = columns(rows)
            take_early(step)
            for group in range(GROUPS):
                take_sub_link(step, 1 - urgent, group)
                multiply_group(now, taken, group, groups[group])
                finish_urgent(group, groups[group])
                send_sub_link(step + 1, urgent, group)
                if group + 1 < GROUPS:
                    stage_others(rows)
            issue(now, [row for _, row in second_list], sets[1])
            issue(now, [row for _, row in third_list], sets[0])
            finish_second(sets[1])
            for group in range(GROUPS):
                send_sub_link(step + 1, 1 - urgent, group)
            for unit in range(UNITS):
                issue(now, unit_rows(unit), sets[(unit + 1) % 2])
                if unit:
                    finish(unit - 1, sets[unit % 2])
                else:
                    finish_third(sets[0])
                    send_reg_links(step + 1)
            finish(UNITS - 1, sets[UNITS % 2])
            return sent(step, carry)

        lax.fori_loop(0, DEG - 1, one_step, 0)

        now = (DEG - 1) % 2
        coeff = coeffs[DEG]

        def finish_own(unit, accs):
            for row, product in zip(unit_rows(unit), products(accs)):
                total[:, row * BLK:(row + 1) * BLK] += coeff * (2.0 * product - cheb[1 - now, row])

        def finish_last(unit, accs):
            for row, product in zip(unit_rows(unit), products(accs)):
                total[:, row * BLK:(row + 1) * BLK] += coeff * (2.0 * product)

        for unit in range(UNITS):
            issue_own(now, unit_rows(unit), sets[unit % 2], unit % 2)
            if unit:
                finish_own(unit - 1, sets[(unit - 1) % 2])
        finish_own(UNITS - 1, sets[(UNITS - 1) % 2])
        stage_others(unit_rows(0))
        taken = columns(unit_rows(0))
        take_early(DEG - 1)
        for group in range(GROUPS):
            take_sub_link(DEG - 1, 1 - urgent, group)
        multiply_staged(now, taken, sets[0])
        for unit in range(UNITS):
            if unit:
                issue_others(now, unit_rows(unit), sets[unit % 2])
                finish_last(unit - 1, sets[(unit - 1) % 2])
        finish_last(UNITS - 1, sets[(UNITS - 1) % 2])

    heights = (2 * PROBES,) * 2 + (2 * PART,) * GROUPS
    pl.run_scoped(run, *[pltpu.ACC(mxu_id=m)((height, 2 * BLK), F32) for height in heights for m in (0, 0, 1, 1)])

    sent(DEG - 1, 0)


def local(probes, blocks, col_slot, send_sub, send_reg, coeffs):
    in_hbm = pl.BlockSpec(memory_space=pltpu.HBM)
    width = ROWS * BLK
    args = (probes, blocks, col_slot.T, send_sub, send_reg, coeffs)
    return pl.pallas_call(
        kernel,
        out_shape=jax.ShapeDtypeStruct((PROBES, width), F32),
        in_specs=[in_hbm] * 6,
        out_specs=pl.BlockSpec(memory_space=pltpu.VMEM),
        scratch_shapes=[
            pltpu.VMEM((PROBES, width), BF16),
            pltpu.VMEM((ROWS, NNZ, BLK, BLK), BF16),
            pltpu.VMEM((ROWS, NNZ, BLK, BLK), BF16),
            pltpu.VMEM((2, ROWS + HALO, PROBES, BLK), BF16),
            pltpu.VMEM((DEG, GROUPS, 2 * HS, PART, BLK), BF16),
            pltpu.VMEM((DEG, 2 * HR, PROBES, BLK), BF16),
            pltpu.VMEM((DEG, GROUPS, 2 * HS, PART, BLK), BF16),
            pltpu.VMEM((DEG, 2 * HR, PROBES, BLK), BF16),
            pltpu.VMEM((2, ROWS, PROBES, BLK), F32),
            pltpu.SMEM((NNZ, ROWS), jnp.int32),
            pltpu.SMEM((1, 2, HS), jnp.int32),
            pltpu.SMEM((1, 2, HR), jnp.int32),
            pltpu.SMEM((DEG + 1,), F32),
            pltpu.SemaphoreType.DMA((UNITS + 1,)),
            pltpu.SemaphoreType.DMA((4,)),
            pltpu.SemaphoreType.DMA((DEG, 2 * GROUPS + 2)),
            pltpu.SemaphoreType.DMA((DEG, 2 * GROUPS + 2)),
        ],
        compiler_params=pltpu.CompilerParams(
            collective_id=0, has_side_effects=True, vmem_limit_bytes=40 << 20
        ),
    )(*(pltpu.with_memory_space_constraint(x, pltpu.HBM) for x in args))


def solution(mesh):
    both = ("region", "sub")
    mapped = jax.shard_map(
        local,
        mesh=mesh,
        in_specs=(
            P(None, both),
            P(both, None, None, None),
            P(both, None),
            P(both, None, None),
            P(both, None, None),
            P(),
        ),
        out_specs=P(None, both),
        check_vma=False,
    )

    def run(*args):
        with jax.sharding.use_abstract_mesh(mesh.abstract_mesh):
            return mapped(*args)

    return run
```
